512 devices in a mesh: rows: 512 (over z, x, y, core).
Axes of the slice: x: 4, y: 8, z: 8, core: 2. Of those that a mesh axis runs over, the one named last changes fastest.
Arguments:
- bases: float32 [5, 524288, 128], P(None, 'rows'), may hold values from -1 to 1
- targets: float32 [524288, 128], P('rows'), may hold values from -8 to 8
Outputs:
- solved: float32 [524288, 128], P('rows')
The draws below stay inside these ranges and needn't reach their ends.
All inputs are finite; a program needn't handle non-finite values.
Results may differ from the reference program's by a relative error of at most 0.0001.
Values sent between devices are 32-bit elements; how exact they have to be, the bound alone decides.
No kernel may reach another device: no remote copies, remote signals or barrier semaphores. Data moves between devices by JAX's collectives and lax.ppermute only.
A program may use at most 64 MiB of HBM per device.

```python
import jax
import jax.numpy as jnp
from jax import lax

K = 128
LEVELS = 5
N = 524288


def noise_field(sub_key, shape):
    return jnp.clip(jax.random.normal(sub_key, shape, jnp.float32), -4.0, 4.0)


def build_fields(key):
    scales = [(0.2 * 2 ** (level_no + 1) / N) ** 0.5 for level_no in range(LEVELS)]
    raw_fields = [noise_field(jax.random.fold_in(key, 100 + level_no), (N, K)) * scales[level_no] for level_no in range(LEVELS)]
    made_bases = []
    for coarse_no in range(LEVELS):
        field = raw_fields[coarse_no]
        for fine_no in range(coarse_no + 1, LEVELS):
            blocks = 2 ** (fine_no + 1)
            factor = (0.1 * scales[coarse_no] ** 2 / (scales[fine_no] ** 2 * K)) ** 0.5
            mixing = noise_field(jax.random.fold_in(key, 200 + 10 * coarse_no + fine_no), (blocks, K, K)) * factor
            nested = jnp.einsum('crk,ckl->crl', raw_fields[fine_no].reshape(blocks, N // blocks, K), mixing, precision=lax.Precision.HIGHEST)
            field = field + nested.reshape(N, K)
        made_bases.append(jnp.clip(field, -1.0, 1.0))
    made_targets = noise_field(jax.random.fold_in(key, 300), (N, K)) * (1.0 / (LEVELS + 1)) ** 0.5
    for fine_no in range(LEVELS):
        blocks = 2 ** (fine_no + 1)
        factor = (1.0 / ((LEVELS + 1) * K * scales[fine_no] ** 2)) ** 0.5
        mixing = noise_field(jax.random.fold_in(key, 400 + fine_no), (blocks, K, K)) * factor
        nested = jnp.einsum('crk,ckl->crl', raw_fields[fine_no].reshape(blocks, N // blocks, K), mixing, precision=lax.Precision.HIGHEST)
        made_targets = made_targets + nested.reshape(N, K)
    return (jnp.stack(made_bases), jnp.clip(made_targets, -8.0, 8.0))


def draw_bases(key, part):
    return build_fields(key)[0]


def draw_targets(key, part):
    return build_fields(key)[1]


def setup_inputs(seed: int = 0) -> dict:
    streams_of = jax.random.split(jax.random.key(seed), 3)
    return {
        "bases": draw_bases(jax.random.fold_in(streams_of[2], 71), 0),
        "targets": draw_targets(jax.random.fold_in(streams_of[2], 71), 0),
    }


def solve_core(left_sums, right_sums):
    identity = jnp.eye(left_sums.shape[-1], dtype=jnp.float32)
    gram_a = left_sums[0]
    gram_b = right_sums[0]
    proj_a = left_sums[1:]
    proj_b = right_sums[1:]
    chol_a = jnp.linalg.cholesky(gram_a)
    inverse_a = jax.scipy.linalg.cho_solve((chol_a, True), identity)
    schur_part = inverse_a - gram_b
    chol_s = jnp.linalg.cholesky(schur_part)
    inverse_s = jax.scipy.linalg.cho_solve((chol_s, True), identity)
    target_b = jnp.einsum('kl,mln->mkn', inverse_a, proj_a, precision=lax.Precision.HIGHEST) - proj_b
    coef_b = jnp.einsum('kl,mln->mkn', inverse_s, target_b, precision=lax.Precision.HIGHEST)
    coef_a = proj_b - jnp.einsum('kl,mln->mkn', gram_b, coef_b, precision=lax.Precision.HIGHEST)
    return (coef_a, coef_b)

def reference(bases, targets):
    n_total = bases.shape[1]
    rank = bases.shape[2]
    fields = [bases[level_no] for level_no in range(LEVELS)] + [targets]
    for level_no in reversed(range(LEVELS)):
        blocks = 2 ** (level_no + 1)
        rows_child = n_total // blocks
        own_basis = fields[level_no].reshape(blocks, rows_child, rank)
        coarser = jnp.stack(fields[:level_no] + [fields[LEVELS]]).reshape(level_no + 1, blocks, rows_child, rank)
        gram = jnp.einsum('crk,crl->ckl', own_basis, own_basis, precision=lax.Precision.HIGHEST)
        proj = jnp.einsum('crk,mcrl->cmkl', own_basis, coarser, precision=lax.Precision.HIGHEST)
        payload = jnp.concatenate([gram[:, None], proj], 1)
        coef_a, coef_b = jax.vmap(solve_core)(payload[0::2], payload[1::2])
        coefs = jnp.stack([coef_a, coef_b], 1).reshape(blocks, level_no + 1, rank, rank)
        corrected = coarser - jnp.einsum('crk,cmkl->mcrl', own_basis, coefs, precision=lax.Precision.HIGHEST)
        corrected = corrected.reshape(level_no + 1, n_total, rank)
        fields = [corrected[m_no] for m_no in range(level_no)] + fields[level_no:LEVELS] + [corrected[level_no]]
    return fields[LEVELS]
```

```python
import functools

import jax
import jax.numpy as jnp
from jax import lax
from jax.experimental import pallas as pl
from jax.experimental.pallas import tpu as pltpu
from jax.sharding import Mesh
from jax.sharding import PartitionSpec as P

LEVELS = 5
K = 128
HALF = K // 2
AXES = ("z", "x", "y", "c")
SIZES = (8, 4, 8, 2)
HIGHEST = lax.Precision.HIGHEST
VMEM_SPEC = pl.BlockSpec(memory_space=pltpu.VMEM)
SMEM_SPEC = pl.BlockSpec(memory_space=pltpu.SMEM)

TOTAL = sum(level_no + 2 for level_no in range(LEVELS))
CHIPS = 8
TILE = HALF // CHIPS


def rows_up_to(level_no):
    return sum(below + 2 for below in range(level_no + 1))


def mm(left, right):
    return jnp.dot(left, right, preferred_element_type=jnp.float32, precision=HIGHEST)


def mtm(left, right):
    return lax.dot_general(
        left,
        right,
        (((0,), (0,)), ((), ())),
        preferred_element_type=jnp.float32,
        precision=HIGHEST,
    )


def two_parts(value):
    high = value.astype(jnp.bfloat16)
    return high, (value - high.astype(jnp.float32)).astype(jnp.bfloat16)


def dot_parts(left, right, dims):
    dot = functools.partial(
        lax.dot_general, dimension_numbers=(dims, ((), ())), preferred_element_type=jnp.float32
    )
    return dot(left[0], right[0]) + (dot(left[0], right[1]) + dot(left[1], right[0]))


def call(body, out_shapes, core, *args, scratch=()):
    outs = pl.pallas_call(
        body,
        out_shape=[jax.ShapeDtypeStruct(shape, jnp.float32) for shape in out_shapes],
        in_specs=[SMEM_SPEC] + [VMEM_SPEC] * len(args),
        out_specs=[VMEM_SPEC] * len(out_shapes),
        scratch_shapes=[pltpu.VMEM(shape, jnp.float32) for shape in scratch],
    )(core, *args)
    return list(outs)


def row_order(level_no):
    return [level_no] + list(range(level_no)) + [LEVELS]


GROUPS = (((4, 3), (4, 3, 2, 1, 0, 5)), ((2, 1), (2, 1, 0, 5)), ((0,), (0, 5)))


def gram_body(core_ref, bases_ref, targets_ref, keep_ref, send_ref, sum_ref):
    step = pl.program_id(0)
    parts = [two_parts(bases_ref[level_no]) for level_no in range(LEVELS)]
    parts.append(two_parts(targets_ref[...]))

    def wide(fields):
        return [jnp.concatenate([parts[m_no][i] for m_no in fields], 1) for i in range(2)]

    starts = {}
    at = 0
    for level_no in reversed(range(LEVELS)):
        starts[level_no] = at
        at += level_no + 2
    for lefts, rights in GROUPS:
        block = dot_parts(wide(lefts), wide(rights), ((0,), (0,)))
        for top, level_no in enumerate(lefts):
            for m_no, field in enumerate(row_order(level_no)):
                to = rights.index(field)
                value = block[top * K : (top + 1) * K, to * K : (to + 1) * K]
                tiles = value.reshape(2, CHIPS, TILE, K)
                at = starts[level_no] + m_no

                @pl.when(step == 0)
                def _():
                    sum_ref[:, :, at] = tiles

                @pl.when(step > 0)
                def _():
                    sum_ref[:, :, at] += tiles

    @pl.when(step == pl.num_programs(0) - 1)
    def _():
        keep_ref[...] = sum_ref[core_ref[0]]
        send_ref[...] = sum_ref[1 - core_ref[0]]


def local_grams(core, bases, targets, block=512):
    rows = bases.shape[1]
    shape = (CHIPS, TOTAL, TILE, K)
    whole = pl.BlockSpec(shape, lambda i: (0, 0, 0, 0))
    return pl.pallas_call(
        gram_body,
        grid=(rows // block,),
        out_shape=[jax.ShapeDtypeStruct(shape, jnp.float32)] * 2,
        in_specs=[
            SMEM_SPEC,
            pl.BlockSpec((LEVELS, block, K), lambda i: (0, i, 0)),
            pl.BlockSpec((block, K), lambda i: (i, 0)),
        ],
        out_specs=[whole, whole],
        scratch_shapes=[pltpu.VMEM((2,) + shape, jnp.float32)],
    )(core, bases, targets)


def inverse_of_complement(product, work_ref):
    row_no = lax.broadcasted_iota(jnp.int32, (K, K), 0)
    column_no = lax.broadcasted_iota(jnp.int32, (K, K), 1)
    eye = (row_no == column_no).astype(jnp.float32)

    def factor(power, inverse):
        power = mm(power, power)
        return power, inverse + mm(inverse, power)

    def size(value):
        return jnp.sum(value * value)

    power, inverse = product, eye + product
    for _ in range(3):
        power, inverse = factor(power, inverse)
    work_ref[0] = power
    work_ref[1] = inverse

    def more(carry):
        step, square = carry
        return (step < 64) & (square * square > 1e-20)

    def body(carry):
        power, inverse = factor(work_ref[0], work_ref[1])
        work_ref[0] = power
        work_ref[1] = inverse
        return carry[0] + 1, size(power)

    lax.while_loop(more, body, (jnp.int32(0), size(power)))
    return work_ref[1]


def solve_pair(gram_own, gram_sib, proj_own, proj_sib, work_ref):
    inverse = inverse_of_complement(mm(gram_sib, gram_own), work_ref)
    coef_own = mm(inverse, proj_sib - mm(gram_sib, proj_own))
    coef_sib = proj_own - mm(gram_own, coef_own)
    return coef_own, coef_sib


def wide_of(ref, first, count):
    return jnp.concatenate([ref[first + m_no] for m_no in range(count)], 1)


def put_wide(ref, first, value):
    for m_no in range(value.shape[1] // K):
        ref[first + m_no] = value[:, m_no * K : (m_no + 1) * K]


def eliminate(level_no, core_no, own, sib, both, next_ref, send_ref, coef_ref, work_ref):
    count = level_no + 1
    proj_own = jnp.concatenate([own(1 + m_no) for m_no in range(count)], 1)
    proj_sib = jnp.concatenate([sib(1 + m_no) for m_no in range(count)], 1)
    coef_own, coef_sib = solve_pair(own(0), sib(0), proj_own, proj_sib, work_ref)
    put_wide(coef_ref, 0, coef_own)
    left = jnp.concatenate([proj_own + coef_sib, proj_sib + coef_own], 0)
    right = jnp.concatenate([coef_own, coef_sib], 0)
    at = 0
    for row_no in reversed(range(level_no)):
        order = [row_no] + list(range(row_no)) + [level_no]
        picked = [right[:, m_no * K : (m_no + 1) * K] for m_no in order]
        row = mtm(left[:, row_no * K : (row_no + 1) * K], jnp.concatenate(picked, 1))
        for m_no in range(row_no + 2):
            next_ref[at] = both(at) - row[:, m_no * K : (m_no + 1) * K]
            at += 1
    if send_ref is not None:
        first = pl.multiple_of(core_no * HALF, HALF)
        for at in range(rows_up_to(level_no - 1)):
            send_ref[at] = next_ref[at, pl.ds(first, HALF)]


def finest_body(core_ref, half_ref, far_ref, next_ref, send_ref, coef_ref, work_ref, all_ref):
    level_no = LEVELS - 1
    core_no = core_ref[0]
    count = level_no + 2
    for at in range(half_ref.shape[1]):
        all_ref[at, pl.ds(pl.multiple_of(core_no * HALF, HALF), HALF)] = half_ref[
            :, at
        ].reshape(HALF, K)
        all_ref[at, pl.ds(pl.multiple_of((1 - core_no) * HALF, HALF), HALF)] = far_ref[
            :, at
        ].reshape(HALF, K)
    eliminate(
        level_no,
        core_no,
        lambda at: all_ref[at],
        lambda at: all_ref[count + at],
        lambda at: all_ref[2 * count + at],
        next_ref,
        send_ref,
        coef_ref,
        work_ref,
    )


def middle_body(level_no, core_ref, own_ref, half_ref, far_ref, next_ref, *refs):
    send_ref, coef_ref, work_ref, sib_ref = refs if len(refs) == 4 else (None,) + refs
    core_no = core_ref[0]
    for at in range(half_ref.shape[0]):
        sib_ref[at, pl.ds(pl.multiple_of(core_no * HALF, HALF), HALF)] = half_ref[at]
        sib_ref[at, pl.ds(pl.multiple_of((1 - core_no) * HALF, HALF), HALF)] = far_ref[at]
    below = level_no + 2
    eliminate(
        level_no,
        core_no,
        lambda at: own_ref[at],
        lambda at: sib_ref[at],
        lambda at: own_ref[below + at] + sib_ref[below + at],
        next_ref,
        send_ref,
        coef_ref,
        work_ref,
    )


def fold_body(level_no, core_ref, coef_ref, *refs):
    finer = LEVELS - 1 - level_no
    coef = wide_of(coef_ref, 0, level_no + 1)
    for at in range(finer):
        old_ref, new_ref = refs[at], refs[finer + at]
        kept = list(range(level_no)) + [level_no + 1]
        old = jnp.concatenate([old_ref[m_no] for m_no in kept], 1)
        put_wide(new_ref, 0, old - mm(old_ref[level_no], coef))


def coarsest_body(core_ref, own_ref, sib_ref, bases_ref, targets_ref, *refs):
    olds, out_ref, work_ref = refs[:-2], refs[-2], refs[-1]
    coef, _ = solve_pair(own_ref[0], sib_ref[0], own_ref[1], sib_ref[1], work_ref)
    mults = [coef]
    for old_ref in reversed(olds):
        mults.append(old_ref[1] - mm(old_ref[0], coef))
    tall = two_parts(jnp.concatenate(mults, 0))
    rows = targets_ref.shape[0]
    block = 256
    for first in range(0, rows, block):
        some = pl.ds(first, block)
        wide = [bases_ref[level_no, some] for level_no in range(LEVELS)]
        wide = two_parts(jnp.concatenate(wide, 1))
        out_ref[some] = targets_ref[some] - dot_parts(wide, tall, ((1,), (0,)))


def swap(value, axis, partner):
    pairs = [(source, partner(source)) for source in range(lax.axis_size(axis))]
    return lax.ppermute(value, axis, pairs)


def swap_cores(value):
    return swap(value, "c", lambda at: at ^ 1)


PARTNERS = {
    4: ("x", lambda at: at ^ 1),
    3: ("x", lambda at: 3 - at),
    2: ("z", lambda at: at ^ 1),
    1: ("z", lambda at: at ^ 2),
    0: ("z", lambda at: (6, 7, 4, 5, 2, 3, 0, 1)[at]),
}
WORK = (2, K, K)


def per_device(bases, targets):
    top = LEVELS - 1
    head = top + 2
    core = lax.axis_index("c").astype(jnp.int32).reshape(1)
    keep, send = local_grams(core, bases, targets)
    part = keep + swap_cores(send)
    part = lax.all_to_all(part, "y", 0, 0).sum(0)
    other = swap(part, *PARTNERS[top])
    piece = jnp.concatenate([part[:head], other[:head], part[head:] + other[head:]], 0)
    half = gather_chips(piece)
    far = swap_cores(half)
    below = rows_up_to(top - 1)
    own, send, coef = call(
        finest_body,
        [(below, K, K), (below, HALF, K), (top + 1, K, K)],
        core,
        half,
        far,
        scratch=[WORK, (piece.shape[0], K, K)],
    )
    mults = [coef]
    for level_no in range(top - 1, 0, -1):
        half = swap(send, *PARTNERS[level_no])
        far = swap_cores(half)
        below = rows_up_to(level_no - 1)
        shapes = [(below, K, K), (below, HALF, K), (level_no + 1, K, K)]
        if level_no == 1:
            del shapes[1]
        outs = call(
            functools.partial(middle_body, level_no),
            shapes,
            core,
            own,
            half,
            far,
            scratch=[WORK, own.shape],
        )
        own, send, coef = outs[0], outs[-2], outs[-1]
        folded = call(
            functools.partial(fold_body, level_no),
            [(level_no + 1, K, K)] * len(mults),
            core,
            coef,
            *mults,
        )
        mults = folded + [coef]
    sib = swap(own, *PARTNERS[0])
    (solved,) = call(
        coarsest_body, [targets.shape], core, own, sib, bases, targets, *mults, scratch=[WORK]
    )
    return solved


def gather_chips(piece):
    return lax.all_gather(piece, "y")


def solution(mesh):
    split = Mesh(mesh.devices.reshape(SIZES), AXES)
    return jax.shard_map(
        per_device,
        mesh=split,
        in_specs=(P(None, AXES, None), P(AXES, None)),
        out_specs=P(AXES, None),
        check_vma=False,
    )
```

```python
import functools

import jax
import jax.numpy as jnp
from jax import lax
from jax.experimental import pallas as pl
from jax.experimental.pallas import tpu as pltpu
from jax.sharding import Mesh
from jax.sharding import PartitionSpec as P

LEVELS = 5
K = 128
HALF = K // 2
AXES = ("z", "x", "y", "c")
SIZES = (8, 4, 8, 2)
HIGHEST = lax.Precision.HIGHEST
VMEM_SPEC = pl.BlockSpec(memory_space=pltpu.VMEM)
SMEM_SPEC = pl.BlockSpec(memory_space=pltpu.SMEM)

TOTAL = sum(level_no + 2 for level_no in range(LEVELS))
CHIPS = 8
TILE = HALF // CHIPS


def rows_up_to(level_no):
    return sum(below + 2 for below in range(level_no + 1))


def mm(left, right):
    return jnp.dot(left, right, preferred_element_type=jnp.float32, precision=HIGHEST)


def mtm(left, right):
    return lax.dot_general(
        left,
        right,
        (((0,), (0,)), ((), ())),
        preferred_element_type=jnp.float32,
        precision=HIGHEST,
    )


def two_parts(value):
    high = value.astype(jnp.bfloat16)
    return high, (value - high.astype(jnp.float32)).astype(jnp.bfloat16)


def dot_parts(left, right, dims):
    dot = functools.partial(
        lax.dot_general, dimension_numbers=(dims, ((), ())), preferred_element_type=jnp.float32
    )
    return dot(left[0], right[0]) + (dot(left[0], right[1]) + dot(left[1], right[0]))


GRANT = pltpu.CompilerParams(vmem_limit_bytes=16 * 2**20)


def call(body, out_shapes, core, *args, scratch=(), after=()):
    used = len(args) + 1

    def whole_body(*refs):
        body(*refs[:used], *refs[used + len(after) :])

    outs = pl.pallas_call(
        whole_body,
        out_shape=[jax.ShapeDtypeStruct(shape, jnp.float32) for shape in out_shapes],
        in_specs=[SMEM_SPEC]
        + [VMEM_SPEC] * len(args)
        + [pl.BlockSpec(memory_space=pl.ANY)] * len(after),
        out_specs=[VMEM_SPEC] * len(out_shapes),
        scratch_shapes=[pltpu.VMEM(shape, jnp.float32) for shape in scratch],
        compiler_params=GRANT,
    )(core, *args, *after)
    return list(outs)


def row_order(level_no):
    return [level_no] + list(range(level_no)) + [LEVELS]


GROUPS = (((4, 3), (4, 3, 2, 1, 0, 5)), ((2, 1), (2, 1, 0, 5)), ((0,), (0, 5)))


def gram_body(core_ref, bases_ref, targets_ref, keep_ref, send_ref):
    first = core_ref[0] == 0
    parts = [two_parts(bases_ref[level_no]) for level_no in range(LEVELS)]
    parts.append(two_parts(targets_ref[...]))

    def wide(fields):
        return [jnp.concatenate([parts[m_no][i] for m_no in fields], 1) for i in range(2)]

    starts = {}
    at = 0
    for level_no in reversed(range(LEVELS)):
        starts[level_no] = at
        at += level_no + 2
    for lefts, rights in GROUPS:
        block = dot_parts(wide(lefts), wide(rights), ((0,), (0,)))
        for top, level_no in enumerate(lefts):
            for m_no, field in enumerate(row_order(level_no)):
                to = rights.index(field)
                value = block[top * K : (top + 1) * K, to * K : (to + 1) * K]
                low = value[:HALF].reshape(CHIPS, TILE, K)
                high = value[HALF:].reshape(CHIPS, TILE, K)
                at = starts[level_no] + m_no
                keep_ref[:, at] = jnp.where(first, low, high)
                send_ref[:, at] = jnp.where(first, high, low)


def local_grams(core, bases, targets):
    shape = (CHIPS, TOTAL, TILE, K)
    return call(gram_body, [shape, shape], core, bases, targets)


def inverse_of_complement(product, work_ref):
    row_no = lax.broadcasted_iota(jnp.int32, (K, K), 0)
    column_no = lax.broadcasted_iota(jnp.int32, (K, K), 1)
    eye = (row_no == column_no).astype(jnp.float32)

    def factor(power, inverse):
        power = mm(power, power)
        return power, inverse + mm(inverse, power)

    def size(value):
        return jnp.sum(value * value)

    power, inverse = product, eye + product
    for _ in range(3):
        power, inverse = factor(power, inverse)
    work_ref[0] = power
    work_ref[1] = inverse

    def more(carry):
        step, square = carry
        return (step < 64) & (square * square > 1e-20)

    def body(carry):
        power, inverse = factor(work_ref[0], work_ref[1])
        work_ref[0] = power
        work_ref[1] = inverse
        return carry[0] + 1, size(power)

    lax.while_loop(more, body, (jnp.int32(0), size(power)))
    return work_ref[1]


def solve_pair(gram_own, gram_sib, proj_own, proj_sib, work_ref):
    inverse = inverse_of_complement(mm(gram_sib, gram_own), work_ref)
    coef_own = mm(inverse, proj_sib - mm(gram_sib, proj_own))
    coef_sib = proj_own - mm(gram_own, coef_own)
    return coef_own, coef_sib


def wide_of(ref, first, count):
    return jnp.concatenate([ref[first + m_no] for m_no in range(count)], 1)


def put_wide(ref, first, value):
    for m_no in range(value.shape[1] // K):
        ref[first + m_no] = value[:, m_no * K : (m_no + 1) * K]


def eliminate(level_no, core_no, own, sib, both, next_ref, send_ref, coef_ref, work_ref):
    count = level_no + 1
    proj_own = jnp.concatenate([own(1 + m_no) for m_no in range(count)], 1)
    proj_sib = jnp.concatenate([sib(1 + m_no) for m_no in range(count)], 1)
    coef_own, coef_sib = solve_pair(own(0), sib(0), proj_own, proj_sib, work_ref)
    put_wide(coef_ref, 0, coef_own)
    left = jnp.concatenate([proj_own + coef_sib, proj_sib + coef_own], 0)
    right = jnp.concatenate([coef_own, coef_sib], 0)
    at = 0
    for row_no in reversed(range(level_no)):
        order = [row_no] + list(range(row_no)) + [level_no]
        picked = [right[:, m_no * K : (m_no + 1) * K] for m_no in order]
        row = mtm(left[:, row_no * K : (row_no + 1) * K], jnp.concatenate(picked, 1))
        for m_no in range(row_no + 2):
            next_ref[at] = both(at) - row[:, m_no * K : (m_no + 1) * K]
            at += 1
    if send_ref is not None:
        first = pl.multiple_of(core_no * HALF, HALF)
        for at in range(rows_up_to(level_no - 1)):
            send_ref[at] = next_ref[at, pl.ds(first, HALF)]


def finest_body(core_ref, half_ref, far_ref, next_ref, send_ref, coef_ref, work_ref, all_ref):
    level_no = LEVELS - 1
    core_no = core_ref[0]
    count = level_no + 2
    for at in range(half_ref.shape[1]):
        all_ref[at, pl.ds(pl.multiple_of(core_no * HALF, HALF), HALF)] = half_ref[
            :, at
        ].reshape(HALF, K)
        all_ref[at, pl.ds(pl.multiple_of((1 - core_no) * HALF, HALF), HALF)] = far_ref[
            :, at
        ].reshape(HALF, K)
    eliminate(
        level_no,
        core_no,
        lambda at: all_ref[at],
        lambda at: all_ref[count + at],
        lambda at: all_ref[2 * count + at],
        next_ref,
        send_ref,
        coef_ref,
        work_ref,
    )


def middle_body(level_no, core_ref, own_ref, half_ref, far_ref, next_ref, *refs):
    send_ref, coef_ref, work_ref, sib_ref = refs if len(refs) == 4 else (None,) + refs
    core_no = core_ref[0]
    for at in range(half_ref.shape[0]):
        sib_ref[at, pl.ds(pl.multiple_of(core_no * HALF, HALF), HALF)] = half_ref[at]
        sib_ref[at, pl.ds(pl.multiple_of((1 - core_no) * HALF, HALF), HALF)] = far_ref[at]
    below = level_no + 2
    eliminate(
        level_no,
        core_no,
        lambda at: own_ref[at],
        lambda at: sib_ref[at],
        lambda at: own_ref[below + at] + sib_ref[below + at],
        next_ref,
        send_ref,
        coef_ref,
        work_ref,
    )


def fold_body(level_no, core_ref, coef_ref, *refs):
    finer = LEVELS - 1 - level_no
    coef = wide_of(coef_ref, 0, level_no + 1)
    for at in range(finer):
        old_ref, new_ref = refs[at], refs[finer + at]
        kept = list(range(level_no)) + [level_no + 1]
        old = jnp.concatenate([old_ref[m_no] for m_no in kept], 1)
        put_wide(new_ref, 0, old - mm(old_ref[level_no], coef))


def tail_body(core_ref, coef_ref, bases_ref, targets_ref, *refs):
    olds, (base_ref, rest_ref) = refs[:-2], refs[-2:]
    coef = wide_of(coef_ref, 0, 2)
    mults = [coef]
    for old_ref in reversed(olds):
        old = jnp.concatenate([old_ref[0], old_ref[2]], 1)
        mults.append(old - mm(old_ref[1], coef))
    tall = two_parts(jnp.concatenate(mults, 0))
    rows = targets_ref.shape[0]
    block = 256
    for first in range(0, rows, block):
        some = pl.ds(first, block)
        wide = [bases_ref[level_no, some] for level_no in range(1, LEVELS)]
        wide = two_parts(jnp.concatenate(wide, 1))
        taken = dot_parts(wide, tall, ((1,), (0,)))
        base_ref[some] = bases_ref[0, some] - taken[:, :K]
        rest_ref[some] = targets_ref[some] - taken[:, K:]


def coarsest_body(core_ref, own_ref, sib_ref, base_ref, rest_ref, out_ref, work_ref):
    inverse = inverse_of_complement(mm(sib_ref[0], own_ref[0]), work_ref)
    coef = mm(inverse, sib_ref[1] - mm(sib_ref[0], own_ref[1]))
    taken = dot_parts(two_parts(base_ref[...]), two_parts(coef), ((1,), (0,)))
    out_ref[...] = rest_ref[...] - taken


def swap(value, axis, partner):
    pairs = [(source, partner(source)) for source in range(lax.axis_size(axis))]
    return lax.ppermute(value, axis, pairs)


def swap_cores(value):
    return swap(value, "c", lambda at: at ^ 1)


PARTNERS = {
    4: ("x", lambda at: at ^ 1),
    3: ("x", lambda at: 3 - at),
    2: ("z", lambda at: at ^ 1),
    1: ("z", lambda at: at ^ 2),
    0: ("z", lambda at: (6, 7, 4, 5, 2, 3, 0, 1)[at]),
}
WORK = (2, K, K)


def per_device(bases, targets):
    top = LEVELS - 1
    head = top + 2
    core = lax.axis_index("c").astype(jnp.int32).reshape(1)
    keep, send = local_grams(core, bases, targets)
    part = keep + swap_cores(send)
    part = lax.all_to_all(part, "y", 0, 0).sum(0)
    other = swap(part, *PARTNERS[top])
    piece = jnp.concatenate([part[:head], other[:head], part[head:] + other[head:]], 0)
    half = gather_chips(piece)
    far = swap_cores(half)
    below = rows_up_to(top - 1)
    own, send, coef = call(
        finest_body,
        [(below, K, K), (below, HALF, K), (top + 1, K, K)],
        core,
        half,
        far,
        scratch=[WORK, (piece.shape[0], K, K)],
    )
    mults = [coef]
    folded = []
    for level_no in range(top - 1, 0, -1):
        half = swap(send, *PARTNERS[level_no])
        far = swap_cores(half)
        below = rows_up_to(level_no - 1)
        shapes = [(below, K, K), (below, HALF, K), (level_no + 1, K, K)]
        if level_no == 1:
            del shapes[1]
        outs = call(
            functools.partial(middle_body, level_no),
            shapes,
            core,
            own,
            half,
            far,
            scratch=[WORK, own.shape],
            after=folded,
        )
        own, send, coef = outs[0], outs[-2], outs[-1]
        if level_no > 1:
            folded = call(
                functools.partial(fold_body, level_no),
                [(level_no + 1, K, K)] * len(mults),
                core,
                coef,
                *mults,
            )
            mults = folded + [coef]
    sib = swap(own, *PARTNERS[0])
    base, rest = call(
        tail_body, [targets.shape, targets.shape], core, coef, bases, targets, *mults
    )
    (solved,) = call(
        coarsest_body, [targets.shape], core, own, sib, base, rest, scratch=[WORK]
    )
    return solved


def gather_chips(piece):
    return lax.all_gather(piece, "y")


def solution(mesh):
    split = Mesh(mesh.devices.reshape(SIZES), AXES)
    return jax.shard_map(
        per_device,
        mesh=split,
        in_specs=(P(None, AXES, None), P(AXES, None)),
        out_specs=P(AXES, None),
        check_vma=False,
    )
```

```python
import functools

import jax
import jax.numpy as jnp
from jax import lax
from jax.experimental import pallas as pl
from jax.experimental.pallas import tpu as pltpu
from jax.sharding import Mesh
from jax.sharding import PartitionSpec as P

LEVELS = 5
K = 128
HALF = K // 2
AXES = ("z", "x", "y", "c")
SIZES = (8, 4, 8, 2)
VMEM_SPEC = pl.BlockSpec(memory_space=pltpu.VMEM)
SMEM_SPEC = pl.BlockSpec(memory_space=pltpu.SMEM)

TOTAL = sum(level_no + 2 for level_no in range(LEVELS))
CHIPS = 8
TILE = HALF // CHIPS


def rows_up_to(level_no):
    return sum(below + 2 for below in range(level_no + 1))


def two_parts(value):
    high = value.astype(jnp.bfloat16)
    return high, (value - high.astype(jnp.float32)).astype(jnp.bfloat16)


def dot_parts(left, right, dims):
    dot = functools.partial(
        lax.dot_general, dimension_numbers=(dims, ((), ())), preferred_element_type=jnp.float32
    )
    return dot(left[0], right[0]) + (dot(left[0], right[1]) + dot(left[1], right[0]))


def mm(left, right):
    return dot_parts(two_parts(left), two_parts(right), ((1,), (0,)))


def mtm(left, right):
    return dot_parts(two_parts(left), two_parts(right), ((0,), (0,)))


GRANT = pltpu.CompilerParams(vmem_limit_bytes=16 * 2**20)


def call(body, out_shapes, core, *args, scratch=(), after=()):
    used = len(args) + 1

    def whole_body(*refs):
        body(*refs[:used], *refs[used + len(after) :])

    outs = pl.pallas_call(
        whole_body,
        out_shape=[jax.ShapeDtypeStruct(shape, jnp.float32) for shape in out_shapes],
        in_specs=[SMEM_SPEC]
        + [VMEM_SPEC] * len(args)
        + [pl.BlockSpec(memory_space=pl.ANY)] * len(after),
        out_specs=[VMEM_SPEC] * len(out_shapes),
        scratch_shapes=[pltpu.VMEM(shape, jnp.float32) for shape in scratch],
        compiler_params=GRANT,
    )(core, *args, *after)
    return list(outs)


def row_order(level_no):
    return [level_no] + list(range(level_no)) + [LEVELS]


GROUPS = (((4, 3), (4, 3, 2, 1, 0, 5)), ((2, 1), (2, 1, 0, 5)), ((0,), (0, 5)))


def gram_body(core_ref, bases_ref, targets_ref, keep_ref, send_ref):
    first = core_ref[0] == 0
    parts = [two_parts(bases_ref[level_no]) for level_no in range(LEVELS)]
    parts.append(two_parts(targets_ref[...]))

    def wide(fields):
        return [jnp.concatenate([parts[m_no][i] for m_no in fields], 1) for i in range(2)]

    starts = {}
    at = 0
    for level_no in reversed(range(LEVELS)):
        starts[level_no] = at
        at += level_no + 2
    for lefts, rights in GROUPS:
        block = dot_parts(wide(lefts), wide(rights), ((0,), (0,)))
        for top, level_no in enumerate(lefts):
            for m_no, field in enumerate(row_order(level_no)):
                to = rights.index(field)
                value = block[top * K : (top + 1) * K, to * K : (to + 1) * K]
                low = value[:HALF].reshape(CHIPS, TILE, K)
                high = value[HALF:].reshape(CHIPS, TILE, K)
                at = starts[level_no] + m_no
                keep_ref[:, at] = jnp.where(first, low, high)
                send_ref[:, at] = jnp.where(first, high, low)


def local_grams(core, bases, targets):
    shape = (CHIPS, TOTAL, TILE, K)
    return call(gram_body, [shape, shape], core, bases, targets)


def inverse_of_complement(product, work_ref):
    row_no = lax.broadcasted_iota(jnp.int32, (K, K), 0)
    column_no = lax.broadcasted_iota(jnp.int32, (K, K), 1)
    eye = (row_no == column_no).astype(jnp.float32)

    def factor(power, inverse):
        power = mm(power, power)
        return power, inverse + mm(inverse, power)

    def size(value):
        return jnp.sum(value * value)

    power, inverse = product, eye + product
    for _ in range(3):
        power, inverse = factor(power, inverse)
    work_ref[0] = power
    work_ref[1] = inverse

    def more(carry):
        step, square = carry
        return (step < 64) & (square * square > 1e-20)

    def body(carry):
        power, inverse = factor(work_ref[0], work_ref[1])
        work_ref[0] = power
        work_ref[1] = inverse
        return carry[0] + 1, size(power)

    lax.while_loop(more, body, (jnp.int32(0), size(power)))
    return work_ref[1]


def solve_pair(gram_own, gram_sib, proj_own, proj_sib, work_ref):
    inverse = inverse_of_complement(mm(gram_sib, gram_own), work_ref)
    coef_own = mm(inverse, proj_sib - mm(gram_sib, proj_own))
    coef_sib = proj_own - mm(gram_own, coef_own)
    return coef_own, coef_sib


def wide_of(ref, first, count):
    return jnp.concatenate([ref[first + m_no] for m_no in range(count)], 1)


def put_wide(ref, first, value):
    for m_no in range(value.shape[1] // K):
        ref[first + m_no] = value[:, m_no * K : (m_no + 1) * K]


def eliminate(level_no, core_no, own, sib, both, next_ref, send_ref, coef_ref, work_ref):
    count = level_no + 1
    proj_own = jnp.concatenate([own(1 + m_no) for m_no in range(count)], 1)
    proj_sib = jnp.concatenate([sib(1 + m_no) for m_no in range(count)], 1)
    coef_own, coef_sib = solve_pair(own(0), sib(0), proj_own, proj_sib, work_ref)
    put_wide(coef_ref, 0, coef_own)
    left = jnp.concatenate([proj_own + coef_sib, proj_sib + coef_own], 0)
    right = jnp.concatenate([coef_own, coef_sib], 0)
    at = 0
    for row_no in reversed(range(level_no)):
        order = [row_no] + list(range(row_no)) + [level_no]
        picked = [right[:, m_no * K : (m_no + 1) * K] for m_no in order]
        row = mtm(left[:, row_no * K : (row_no + 1) * K], jnp.concatenate(picked, 1))
        for m_no in range(row_no + 2):
            next_ref[at] = both(at) - row[:, m_no * K : (m_no + 1) * K]
            at += 1
    if send_ref is not None:
        first = pl.multiple_of(core_no * HALF, HALF)
        for at in range(rows_up_to(level_no - 1)):
            send_ref[at] = next_ref[at, pl.ds(first, HALF)]


def finest_body(core_ref, half_ref, far_ref, next_ref, send_ref, coef_ref, work_ref, all_ref):
    level_no = LEVELS - 1
    core_no = core_ref[0]
    count = level_no + 2
    for at in range(half_ref.shape[1]):
        all_ref[at, pl.ds(pl.multiple_of(core_no * HALF, HALF), HALF)] = half_ref[
            :, at
        ].reshape(HALF, K)
        all_ref[at, pl.ds(pl.multiple_of((1 - core_no) * HALF, HALF), HALF)] = far_ref[
            :, at
        ].reshape(HALF, K)
    eliminate(
        level_no,
        core_no,
        lambda at: all_ref[at],
        lambda at: all_ref[count + at],
        lambda at: all_ref[2 * count + at],
        next_ref,
        send_ref,
        coef_ref,
        work_ref,
    )


def middle_body(level_no, core_ref, own_ref, half_ref, far_ref, next_ref, *refs):
    send_ref, coef_ref, work_ref, sib_ref = refs if len(refs) == 4 else (None,) + refs
    core_no = core_ref[0]
    for at in range(half_ref.shape[0]):
        sib_ref[at, pl.ds(pl.multiple_of(core_no * HALF, HALF), HALF)] = half_ref[at]
        sib_ref[at, pl.ds(pl.multiple_of((1 - core_no) * HALF, HALF), HALF)] = far_ref[at]
    below = level_no + 2
    eliminate(
        level_no,
        core_no,
        lambda at: own_ref[at],
        lambda at: sib_ref[at],
        lambda at: own_ref[below + at] + sib_ref[below + at],
        next_ref,
        send_ref,
        coef_ref,
        work_ref,
    )


def fold_body(level_no, core_ref, coef_ref, *refs):
    finer = LEVELS - 1 - level_no
    coef = wide_of(coef_ref, 0, level_no + 1)
    for at in range(finer):
        old_ref, new_ref = refs[at], refs[finer + at]
        kept = list(range(level_no)) + [level_no + 1]
        old = jnp.concatenate([old_ref[m_no] for m_no in kept], 1)
        put_wide(new_ref, 0, old - mm(old_ref[level_no], coef))


def tail_body(core_ref, coef_ref, bases_ref, targets_ref, *refs):
    olds, (base_ref, rest_ref) = refs[:-2], refs[-2:]
    coef = wide_of(coef_ref, 0, 2)
    mults = [coef]
    for old_ref in reversed(olds):
        old = jnp.concatenate([old_ref[0], old_ref[2]], 1)
        mults.append(old - mm(old_ref[1], coef))
    tall = two_parts(jnp.concatenate(mults, 0))
    rows = targets_ref.shape[0]
    block = 256
    for first in range(0, rows, block):
        some = pl.ds(first, block)
        wide = [bases_ref[level_no, some] for level_no in range(1, LEVELS)]
        wide = two_parts(jnp.concatenate(wide, 1))
        taken = dot_parts(wide, tall, ((1,), (0,)))
        base_ref[some] = bases_ref[0, some] - taken[:, :K]
        rest_ref[some] = targets_ref[some] - taken[:, K:]


def coarsest_body(core_ref, own_ref, sib_ref, base_ref, rest_ref, out_ref, work_ref):
    inverse = inverse_of_complement(mm(sib_ref[0], own_ref[0]), work_ref)
    coef = mm(inverse, sib_ref[1] - mm(sib_ref[0], own_ref[1]))
    taken = dot_parts(two_parts(base_ref[...]), two_parts(coef), ((1,), (0,)))
    out_ref[...] = rest_ref[...] - taken


def swap(value, axis, partner):
    pairs = [(source, partner(source)) for source in range(lax.axis_size(axis))]
    return lax.ppermute(value, axis, pairs)


def swap_cores(value):
    return swap(value, "c", lambda at: at ^ 1)


PARTNERS = {
    4: ("x", lambda at: at ^ 1),
    3: ("x", lambda at: 3 - at),
    2: ("z", lambda at: at ^ 1),
    1: ("z", lambda at: at ^ 2),
    0: ("z", lambda at: (6, 7, 4, 5, 2, 3, 0, 1)[at]),
}
WORK = (2, K, K)


def per_device(bases, targets):
    top = LEVELS - 1
    head = top + 2
    core = lax.axis_index("c").astype(jnp.int32).reshape(1)
    keep, send = local_grams(core, bases, targets)
    part = keep + swap_cores(send)
    part = lax.all_to_all(part, "y", 0, 0).sum(0)
    other = swap(part, *PARTNERS[top])
    piece = jnp.concatenate([part[:head], other[:head], part[head:] + other[head:]], 0)
    half = gather_chips(piece)
    far = swap_cores(half)
    below = rows_up_to(top - 1)
    own, send, coef = call(
        finest_body,
        [(below, K, K), (below, HALF, K), (top + 1, K, K)],
        core,
        half,
        far,
        scratch=[WORK, (piece.shape[0], K, K)],
    )
    mults = [coef]
    folded = []
    for level_no in range(top - 1, 0, -1):
        half = swap(send, *PARTNERS[level_no])
        far = swap_cores(half)
        below = rows_up_to(level_no - 1)
        shapes = [(below, K, K), (below, HALF, K), (level_no + 1, K, K)]
        if level_no == 1:
            del shapes[1]
        outs = call(
            functools.partial(middle_body, level_no),
            shapes,
            core,
            own,
            half,
            far,
            scratch=[WORK, own.shape],
            after=folded,
        )
        own, send, coef = outs[0], outs[-2], outs[-1]
        if level_no > 1:
            folded = call(
                functools.partial(fold_body, level_no),
                [(level_no + 1, K, K)] * len(mults),
                core,
                coef,
                *mults,
            )
            mults = folded + [coef]
    sib = swap(own, *PARTNERS[0])
    base, rest = call(
        tail_body, [targets.shape, targets.shape], core, coef, bases, targets, *mults
    )
    (solved,) = call(
        coarsest_body, [targets.shape], core, own, sib, base, rest, scratch=[WORK]
    )
    return solved


def gather_chips(piece):
    return lax.all_gather(piece, "y")


def solution(mesh):
    split = Mesh(mesh.devices.reshape(SIZES), AXES)
    return jax.shard_map(
        per_device,
        mesh=split,
        in_specs=(P(None, AXES, None), P(AXES, None)),
        out_specs=P(AXES, None),
        check_vma=False,
    )
```

```python
import functools

import jax
import jax.numpy as jnp
from jax import lax
from jax.experimental import pallas as pl
from jax.experimental.pallas import tpu as pltpu
from jax.sharding import Mesh
from jax.sharding import PartitionSpec as P

LEVELS = 5
K = 128
HALF = K // 2
AXES = ("z", "x", "y", "c")
SIZES = (8, 4, 8, 2)
VMEM_SPEC = pl.BlockSpec(memory_space=pltpu.VMEM)
SMEM_SPEC = pl.BlockSpec(memory_space=pltpu.SMEM)

CHIPS = 8
TILE = HALF // CHIPS
TOTAL = 18


def rows_up_to(level_no):
    return sum(below + 2 for below in range(level_no + 1))


def row_order(level_no):
    return [level_no] + list(range(level_no)) + [LEVELS]


def packed_order(level_no):
    tops = [level_no] if level_no % 2 else [level_no - 1]
    pairs = [("pair", top, top - 1) for top in range(tops[0], 0, -2)]
    diagonals = pairs if level_no % 2 else [("one", level_no)] + pairs
    others = [
        [(row_no, m_no) for m_no in row_order(row_no)[1:]]
        for row_no in reversed(range(level_no + 1))
    ]
    return diagonals[:1] + others[0] + diagonals[1:] + sum(others[1:], [])


def full_index(level_no, row_no, m_no):
    above = sum(row + 2 for row in range(row_no + 1, level_no + 1))
    return above + row_order(row_no).index(m_no)


def grid_of(rows, first=0):
    row_no = lax.broadcasted_iota(jnp.int32, (rows, K), 0) + first
    return row_no, lax.broadcasted_iota(jnp.int32, (rows, K), 1)


def diagonal_of(matrix):
    row_no, column_no = grid_of(K)
    return jnp.sum(jnp.where(row_no == column_no, matrix, 0.0), 0, keepdims=True)


def from_lower(packed):
    row_no, column_no = grid_of(K)
    strict = jnp.where(column_no < row_no, packed, 0.0)
    return jnp.where(column_no <= row_no, packed, 0.0) + strict.T


def from_upper(packed, diagonal):
    row_no, column_no = grid_of(K)
    strict = jnp.where(column_no > row_no, packed, 0.0)
    return strict + strict.T + jnp.where(column_no == row_no, diagonal, 0.0)


def two_parts(value):
    high = value.astype(jnp.bfloat16)
    return high, (value - high.astype(jnp.float32)).astype(jnp.bfloat16)


def dot_parts(left, right, dims):
    dot = functools.partial(
        lax.dot_general, dimension_numbers=(dims, ((), ())), preferred_element_type=jnp.float32
    )
    return dot(left[0], right[0]) + (dot(left[0], right[1]) + dot(left[1], right[0]))


def mm(left, right):
    return dot_parts(two_parts(left), two_parts(right), ((1,), (0,)))


def mtm(left, right):
    return dot_parts(two_parts(left), two_parts(right), ((0,), (0,)))


GRANT = pltpu.CompilerParams(vmem_limit_bytes=16 * 2**20)


def call(body, out_shapes, core, *args, scratch=(), after=()):
    used = len(args) + 1

    def whole_body(*refs):
        body(*refs[:used], *refs[used + len(after) :])

    outs = pl.pallas_call(
        whole_body,
        out_shape=[jax.ShapeDtypeStruct(shape, jnp.float32) for shape in out_shapes],
        in_specs=[SMEM_SPEC]
        + [VMEM_SPEC] * len(args)
        + [pl.BlockSpec(memory_space=pl.ANY)] * len(after),
        out_specs=[VMEM_SPEC] * len(out_shapes),
        scratch_shapes=[pltpu.VMEM(shape, jnp.float32) for shape in scratch],
        compiler_params=GRANT,
    )(core, *args, *after)
    return list(outs)


GROUPS = (((4, 3), (4, 3, 2, 1, 0, 5)), ((2, 1), (2, 1, 0, 5)), ((0,), (0, 5)))


def hidden_diagonals(made):
    row_no, column_no = grid_of(K)
    out = jnp.zeros((K, K), jnp.float32)
    for pair_no, level_no in enumerate((2, 0)):
        diagonal = jnp.broadcast_to(diagonal_of(made[level_no, level_no]), (K, K))
        left = pltpu.roll(diagonal, HALF, 1)
        out = jnp.where(row_no == 2 * pair_no, left, out)
        out = jnp.where(row_no == 2 * pair_no + 1, diagonal, out)
    return jnp.where(column_no >= HALF, out, 0.0)


def found_diagonals(packed):
    _, column_no = grid_of(8)
    found = []
    for pair_no in range(2):
        left = jnp.broadcast_to(packed[2 * pair_no : 2 * pair_no + 1], (8, K))
        right = jnp.broadcast_to(packed[2 * pair_no + 1 : 2 * pair_no + 2], (8, K))
        both = jnp.where(column_no < HALF, pltpu.roll(left, HALF, 1), right)
        found.append(both[:1])
    return found


def gram_body(core_ref, bases_ref, targets_ref, keep_ref, send_ref):
    first = core_ref[0] == 0
    parts = [two_parts(bases_ref[level_no]) for level_no in range(LEVELS)]
    parts.append(two_parts(targets_ref[...]))

    def wide(fields):
        return [jnp.concatenate([parts[m_no][i] for m_no in fields], 1) for i in range(2)]

    made = {}
    for lefts, rights in GROUPS:
        block = dot_parts(wide(lefts), wide(rights), ((0,), (0,)))
        for top, level_no in enumerate(lefts):
            for field in row_order(level_no):
                to = rights.index(field)
                made[level_no, field] = block[top * K : (top + 1) * K, to * K : (to + 1) * K]
    row_no, column_no = grid_of(K)
    lower = column_no <= row_no
    for at, entry in enumerate(packed_order(LEVELS - 1)):
        if entry[0] == "one":
            value = jnp.where(lower, made[entry[1], entry[1]], hidden_diagonals(made))
        elif entry[0] == "pair":
            value = jnp.where(lower, made[entry[1], entry[1]], made[entry[2], entry[2]])
        else:
            value = made[entry]
        low = value[:HALF].reshape(CHIPS, TILE, K)
        high = value[HALF:].reshape(CHIPS, TILE, K)
        keep_ref[:, at] = jnp.where(first, low, high)
        send_ref[:, at] = jnp.where(first, high, low)


def local_grams(core, bases, targets):
    shape = (CHIPS, TOTAL, TILE, K)
    return call(gram_body, [shape, shape], core, bases, targets)


def inverse_of_complement(product, work_ref):
    row_no = lax.broadcasted_iota(jnp.int32, (K, K), 0)
    column_no = lax.broadcasted_iota(jnp.int32, (K, K), 1)
    eye = (row_no == column_no).astype(jnp.float32)

    def factor(power, inverse):
        power = mm(power, power)
        return power, inverse + mm(inverse, power)

    def size(value):
        return jnp.sum(value * value)

    power, inverse = product, eye + product
    for _ in range(3):
        power, inverse = factor(power, inverse)
    work_ref[0] = power
    work_ref[1] = inverse

    def more(carry):
        step, square = carry
        return (step < 64) & (square * square > 1e-20)

    def body(carry):
        power, inverse = factor(work_ref[0], work_ref[1])
        work_ref[0] = power
        work_ref[1] = inverse
        return carry[0] + 1, size(power)

    lax.while_loop(more, body, (jnp.int32(0), size(power)))
    return work_ref[1]


def solve_pair(gram_own, gram_sib, proj_own, proj_sib, work_ref):
    inverse = inverse_of_complement(mm(gram_sib, gram_own), work_ref)
    coef_own = mm(inverse, proj_sib - mm(gram_sib, proj_own))
    coef_sib = proj_own - mm(gram_own, coef_own)
    return coef_own, coef_sib


def wide_of(ref, first, count):
    return jnp.concatenate([ref[first + m_no] for m_no in range(count)], 1)


def put_wide(ref, first, value):
    for m_no in range(value.shape[1] // K):
        ref[first + m_no] = value[:, m_no * K : (m_no + 1) * K]


def eliminate(level_no, core_no, own, sib, both, next_ref, send_ref, coef_ref, work_ref):
    count = level_no + 1
    proj_own = jnp.concatenate([own(1 + m_no) for m_no in range(count)], 1)
    proj_sib = jnp.concatenate([sib(1 + m_no) for m_no in range(count)], 1)
    coef_own, coef_sib = solve_pair(own(0), sib(0), proj_own, proj_sib, work_ref)
    put_wide(coef_ref, 0, coef_own)
    left = jnp.concatenate([proj_own + coef_sib, proj_sib + coef_own], 0)
    right = jnp.concatenate([coef_own, coef_sib], 0)
    at = 0
    for row_no in reversed(range(level_no)):
        order = [row_no] + list(range(row_no)) + [level_no]
        picked = [right[:, m_no * K : (m_no + 1) * K] for m_no in order]
        row = mtm(left[:, row_no * K : (row_no + 1) * K], jnp.concatenate(picked, 1))
        for m_no, field in enumerate(row_order(row_no)):
            next_ref[at] = both(row_no, field) - row[:, m_no * K : (m_no + 1) * K]
            at += 1
    if send_ref is not None:
        below = level_no - 1
        first = pl.multiple_of(core_no * HALF, HALF)
        row_no, column_no = grid_of(HALF, first)
        extra = jnp.zeros((8, K), jnp.float32)
        extra_row, _ = grid_of(8)
        extras = 0

        def some(row, m_no):
            return next_ref[full_index(below, row, m_no), pl.ds(first, HALF)]

        entries = packed_order(below)
        for at, entry in enumerate(entries):
            if entry[0] == "one":
                value = some(entry[1], entry[1])
            elif entry[0] == "pair":
                value = jnp.where(
                    column_no <= row_no,
                    some(entry[1], entry[1]),
                    some(entry[2], entry[2]),
                )
                lost = next_ref[full_index(below, entry[2], entry[2])]
                extra = jnp.where(extra_row == extras, diagonal_of(lost), extra)
                extras += 1
            else:
                value = some(*entry)
            send_ref[at * HALF : (at + 1) * HALF] = value
        send_ref[len(entries) * HALF :] = extra


def unpack(level_no, order, packed_ref, base, diagonals):
    found = {}
    pairs = 0
    for at, entry in enumerate(order):
        value = packed_ref[base + at]
        if entry[0] == "one":
            found[entry[1], entry[1]] = value
        elif entry[0] == "pair":
            found[entry[1], entry[1]] = from_lower(value)
            found[entry[2], entry[2]] = from_upper(value, diagonals[pairs])
            pairs += 1
        else:
            found[entry] = value
    return found


def join_halves(core_no, count, half_ref, far_ref, packed_ref, half_of):
    own = pl.ds(pl.multiple_of(core_no * HALF, HALF), HALF)
    far = pl.ds(pl.multiple_of((1 - core_no) * HALF, HALF), HALF)
    for at in range(count):
        packed_ref[at, own] = half_of(half_ref, at)
        packed_ref[at, far] = half_of(far_ref, at)


def finest_body(
    core_ref, half_ref, far_ref, next_ref, send_ref, coef_ref, work_ref, packed_ref
):
    level_no = LEVELS - 1
    core_no = core_ref[0]
    count = level_no + 2
    join_halves(
        core_no,
        half_ref.shape[1],
        half_ref,
        far_ref,
        packed_ref,
        lambda ref, at: ref[:, at].reshape(HALF, K),
    )
    diagonals = found_diagonals(packed_ref[0] + packed_ref[count])
    order = packed_order(level_no)
    both = unpack(level_no, order[count:], packed_ref, 2 * count, diagonals)
    eliminate(
        level_no,
        core_no,
        lambda m_no: packed_ref[m_no] if m_no else from_lower(packed_ref[0]),
        lambda m_no: packed_ref[count + m_no] if m_no else from_lower(packed_ref[count]),
        lambda row_no, field: both[row_no, field],
        next_ref,
        send_ref,
        coef_ref,
        work_ref,
    )


def middle_body(level_no, core_ref, own_ref, half_ref, far_ref, next_ref, *refs):
    send_ref, coef_ref, work_ref, packed_ref = refs if len(refs) == 4 else (None,) + refs
    core_no = core_ref[0]
    order = packed_order(level_no)
    join_halves(
        core_no,
        len(order),
        half_ref,
        far_ref,
        packed_ref,
        lambda ref, at: ref[at * HALF : (at + 1) * HALF],
    )
    tail = half_ref[len(order) * HALF :]
    found = unpack(level_no, order, packed_ref, 0, (tail[0:1], tail[1:2]))
    fields = row_order(level_no)
    eliminate(
        level_no,
        core_no,
        lambda m_no: own_ref[m_no],
        lambda m_no: found[level_no, fields[m_no]],
        lambda row_no, field: own_ref[full_index(level_no, row_no, field)]
        + found[row_no, field],
        next_ref,
        send_ref,
        coef_ref,
        work_ref,
    )


def fold_body(level_no, core_ref, coef_ref, *refs):
    finer = LEVELS - 1 - level_no
    coef = wide_of(coef_ref, 0, level_no + 1)
    for at in range(finer):
        old_ref, new_ref = refs[at], refs[finer + at]
        kept = list(range(level_no)) + [level_no + 1]
        old = jnp.concatenate([old_ref[m_no] for m_no in kept], 1)
        put_wide(new_ref, 0, old - mm(old_ref[level_no], coef))


def tail_body(core_ref, coef_ref, bases_ref, targets_ref, *refs):
    olds, (base_ref, rest_ref) = refs[:-2], refs[-2:]
    coef = wide_of(coef_ref, 0, 2)
    mults = [coef]
    for old_ref in reversed(olds):
        old = jnp.concatenate([old_ref[0], old_ref[2]], 1)
        mults.append(old - mm(old_ref[1], coef))
    tall = two_parts(jnp.concatenate(mults, 0))
    rows = targets_ref.shape[0]
    block = 256
    for first in range(0, rows, block):
        some = pl.ds(first, block)
        wide = [bases_ref[level_no, some] for level_no in range(1, LEVELS)]
        wide = two_parts(jnp.concatenate(wide, 1))
        taken = dot_parts(wide, tall, ((1,), (0,)))
        base_ref[some] = bases_ref[0, some] - taken[:, :K]
        rest_ref[some] = targets_ref[some] - taken[:, K:]


def coarsest_body(core_ref, own_ref, sib_ref, base_ref, rest_ref, out_ref, work_ref):
    inverse = inverse_of_complement(mm(sib_ref[0], own_ref[0]), work_ref)
    coef = mm(inverse, sib_ref[1] - mm(sib_ref[0], own_ref[1]))
    taken = dot_parts(two_parts(base_ref[...]), two_parts(coef), ((1,), (0,)))
    out_ref[...] = rest_ref[...] - taken


def swap(value, axis, partner):
    pairs = [(source, partner(source)) for source in range(lax.axis_size(axis))]
    return lax.ppermute(value, axis, pairs)


def swap_cores(value):
    return swap(value, "c", lambda at: at ^ 1)


PARTNERS = {
    4: ("x", lambda at: at ^ 1),
    3: ("x", lambda at: 3 - at),
    2: ("z", lambda at: at ^ 1),
    1: ("z", lambda at: at ^ 2),
    0: ("z", lambda at: (6, 7, 4, 5, 2, 3, 0, 1)[at]),
}
WORK = (2, K, K)


def sent_shape(level_no):
    return (len(packed_order(level_no)) * HALF + 8, K)


def per_device(bases, targets):
    top = LEVELS - 1
    head = top + 2
    core = lax.axis_index("c").astype(jnp.int32).reshape(1)
    keep, send = local_grams(core, bases, targets)
    part = keep + swap_cores(send)
    part = lax.all_to_all(part, "y", 0, 0).sum(0)
    other = swap(part, *PARTNERS[top])
    piece = jnp.concatenate([part[:head], other[:head], part[head:] + other[head:]], 0)
    half = gather_chips(piece)
    far = swap_cores(half)
    below = rows_up_to(top - 1)
    own, send, coef = call(
        finest_body,
        [(below, K, K), sent_shape(top - 1), (top + 1, K, K)],
        core,
        half,
        far,
        scratch=[WORK, (piece.shape[0], K, K)],
    )
    mults = [coef]
    folded = []
    for level_no in range(top - 1, 0, -1):
        half = swap(send, *PARTNERS[level_no])
        far = swap_cores(half)
        below = rows_up_to(level_no - 1)
        shapes = [(below, K, K), sent_shape(level_no - 1), (level_no + 1, K, K)]
        if level_no == 1:
            del shapes[1]
        outs = call(
            functools.partial(middle_body, level_no),
            shapes,
            core,
            own,
            half,
            far,
            scratch=[WORK, (len(packed_order(level_no)), K, K)],
            after=folded,
        )
        own, send, coef = outs[0], outs[-2], outs[-1]
        if level_no > 1:
            folded = call(
                functools.partial(fold_body, level_no),
                [(level_no + 1, K, K)] * len(mults),
                core,
                coef,
                *mults,
            )
            mults = folded + [coef]
    sib = swap(own, *PARTNERS[0])
    base, rest = call(
        tail_body, [targets.shape, targets.shape], core, coef, bases, targets, *mults
    )
    (solved,) = call(
        coarsest_body, [targets.shape], core, own, sib, base, rest, scratch=[WORK]
    )
    return solved


def gather_chips(piece):
    return lax.all_gather(piece, "y")


def solution(mesh):
    split = Mesh(mesh.devices.reshape(SIZES), AXES)
    return jax.shard_map(
        per_device,
        mesh=split,
        in_specs=(P(None, AXES, None), P(AXES, None)),
        out_specs=P(AXES, None),
        check_vma=False,
    )
```

```python
import functools

import jax
import jax.numpy as jnp
from jax import lax
from jax.experimental import pallas as pl
from jax.experimental.pallas import tpu as pltpu
from jax.sharding import Mesh
from jax.sharding import PartitionSpec as P

LEVELS = 5
K = 128
HALF = K // 2
AXES = ("z", "x", "y", "c")
SIZES = (8, 4, 8, 2)
VMEM_SPEC = pl.BlockSpec(memory_space=pltpu.VMEM)
SMEM_SPEC = pl.BlockSpec(memory_space=pltpu.SMEM)

CHIPS = 8
TILE = HALF // CHIPS
TOTAL = 18


def rows_up_to(level_no):
    return sum(below + 2 for below in range(level_no + 1))


def row_order(level_no):
    return [level_no] + list(range(level_no)) + [LEVELS]


def packed_order(level_no):
    tops = [level_no] if level_no % 2 else [level_no - 1]
    pairs = [("pair", top, top - 1) for top in range(tops[0], 0, -2)]
    diagonals = pairs if level_no % 2 else [("one", level_no)] + pairs
    others = [
        [(row_no, m_no) for m_no in row_order(row_no)[1:]]
        for row_no in reversed(range(level_no + 1))
    ]
    return diagonals[:1] + others[0] + diagonals[1:] + sum(others[1:], [])


def full_index(level_no, row_no, m_no):
    above = sum(row + 2 for row in range(row_no + 1, level_no + 1))
    return above + row_order(row_no).index(m_no)


def grid_of(rows, first=0):
    row_no = lax.broadcasted_iota(jnp.int32, (rows, K), 0) + first
    return row_no, lax.broadcasted_iota(jnp.int32, (rows, K), 1)


def diagonal_of(matrix):
    row_no, column_no = grid_of(K)
    return jnp.sum(jnp.where(row_no == column_no, matrix, 0.0), 0, keepdims=True)


def from_lower(packed):
    row_no, column_no = grid_of(K)
    strict = jnp.where(column_no < row_no, packed, 0.0)
    return jnp.where(column_no <= row_no, packed, 0.0) + strict.T


def from_upper(packed, diagonal):
    row_no, column_no = grid_of(K)
    strict = jnp.where(column_no > row_no, packed, 0.0)
    return strict + strict.T + jnp.where(column_no == row_no, diagonal, 0.0)


def two_parts(value):
    high = value.astype(jnp.bfloat16)
    return high, (value - high.astype(jnp.float32)).astype(jnp.bfloat16)


def dot_parts(left, right, dims):
    dot = functools.partial(
        lax.dot_general, dimension_numbers=(dims, ((), ())), preferred_element_type=jnp.float32
    )
    return dot(left[0], right[0]) + (dot(left[0], right[1]) + dot(left[1], right[0]))


def mm(left, right):
    return dot_parts(two_parts(left), two_parts(right), ((1,), (0,)))


def mtm(left, right):
    return dot_parts(two_parts(left), two_parts(right), ((0,), (0,)))


GRANT = pltpu.CompilerParams(vmem_limit_bytes=16 * 2**20)


def call(body, out_shapes, core, *args, scratch=(), after=()):
    used = len(args) + 1

    def whole_body(*refs):
        body(*refs[:used], *refs[used + len(after) :])

    outs = pl.pallas_call(
        whole_body,
        out_shape=[jax.ShapeDtypeStruct(shape, jnp.float32) for shape in out_shapes],
        in_specs=[SMEM_SPEC]
        + [VMEM_SPEC] * len(args)
        + [pl.BlockSpec(memory_space=pl.ANY)] * len(after),
        out_specs=[VMEM_SPEC] * len(out_shapes),
        scratch_shapes=[pltpu.VMEM(shape, jnp.float32) for shape in scratch],
        compiler_params=GRANT,
    )(core, *args, *after)
    return list(outs)


GROUPS = (((4, 3), (4, 3, 2, 1, 0, 5)), ((2, 1), (2, 1, 0, 5)), ((0,), (0, 5)))


def hidden_diagonals(made):
    row_no, column_no = grid_of(K)
    out = jnp.zeros((K, K), jnp.float32)
    for pair_no, level_no in enumerate((2, 0)):
        diagonal = jnp.broadcast_to(diagonal_of(made[level_no, level_no]), (K, K))
        left = pltpu.roll(diagonal, HALF, 1)
        out = jnp.where(row_no == 2 * pair_no, left, out)
        out = jnp.where(row_no == 2 * pair_no + 1, diagonal, out)
    return jnp.where(column_no >= HALF, out, 0.0)


def found_diagonals(packed):
    _, column_no = grid_of(8)
    found = []
    for pair_no in range(2):
        left = jnp.broadcast_to(packed[2 * pair_no : 2 * pair_no + 1], (8, K))
        right = jnp.broadcast_to(packed[2 * pair_no + 1 : 2 * pair_no + 2], (8, K))
        both = jnp.where(column_no < HALF, pltpu.roll(left, HALF, 1), right)
        found.append(both[:1])
    return found


def gram_body(core_ref, bases_ref, targets_ref, keep_ref, send_ref):
    first = core_ref[0] == 0
    parts = [two_parts(bases_ref[level_no]) for level_no in range(LEVELS)]
    parts.append(two_parts(targets_ref[...]))

    def wide(fields):
        return [jnp.concatenate([parts[m_no][i] for m_no in fields], 1) for i in range(2)]

    made = {}
    for lefts, rights in GROUPS:
        block = dot_parts(wide(lefts), wide(rights), ((0,), (0,)))
        for top, level_no in enumerate(lefts):
            for field in row_order(level_no):
                to = rights.index(field)
                made[level_no, field] = block[top * K : (top + 1) * K, to * K : (to + 1) * K]
    row_no, column_no = grid_of(K)
    lower = column_no <= row_no
    for at, entry in enumerate(packed_order(LEVELS - 1)):
        if entry[0] == "one":
            value = jnp.where(lower, made[entry[1], entry[1]], hidden_diagonals(made))
        elif entry[0] == "pair":
            value = jnp.where(lower, made[entry[1], entry[1]], made[entry[2], entry[2]])
        else:
            value = made[entry]
        low = value[:HALF].reshape(CHIPS, TILE, K)
        high = value[HALF:].reshape(CHIPS, TILE, K)
        keep_ref[:, at] = jnp.where(first, low, high)
        send_ref[:, at] = jnp.where(first, high, low)


def local_grams(core, bases, targets):
    shape = (CHIPS, TOTAL, TILE, K)
    return call(gram_body, [shape, shape], core, bases, targets)


def inverse_of_complement(product, work_ref):
    row_no = lax.broadcasted_iota(jnp.int32, (K, K), 0)
    column_no = lax.broadcasted_iota(jnp.int32, (K, K), 1)
    eye = (row_no == column_no).astype(jnp.float32)

    def factor(power, inverse):
        power = mm(power, power)
        return power, inverse + mm(inverse, power)

    def size(value):
        return jnp.sum(value * value)

    power, inverse = product, eye + product
    for _ in range(3):
        power, inverse = factor(power, inverse)
    work_ref[0] = power
    work_ref[1] = inverse

    def more(carry):
        step, square = carry
        return (step < 64) & (square * square > 1e-20)

    def body(carry):
        power, inverse = factor(work_ref[0], work_ref[1])
        work_ref[0] = power
        work_ref[1] = inverse
        return carry[0] + 1, size(power)

    lax.while_loop(more, body, (jnp.int32(0), size(power)))
    return work_ref[1]


def solve_pair(gram_own, gram_sib, proj_own, proj_sib, work_ref):
    inverse = inverse_of_complement(mm(gram_sib, gram_own), work_ref)
    coef_own = mm(inverse, proj_sib - mm(gram_sib, proj_own))
    coef_sib = proj_own - mm(gram_own, coef_own)
    return coef_own, coef_sib


def wide_of(ref, first, count):
    return jnp.concatenate([ref[first + m_no] for m_no in range(count)], 1)


def put_wide(ref, first, value):
    for m_no in range(value.shape[1] // K):
        ref[first + m_no] = value[:, m_no * K : (m_no + 1) * K]


def eliminate(level_no, core_no, own, sib, both, next_ref, send_ref, coef_ref, work_ref):
    count = level_no + 1
    proj_own = jnp.concatenate([own(1 + m_no) for m_no in range(count)], 1)
    proj_sib = jnp.concatenate([sib(1 + m_no) for m_no in range(count)], 1)
    coef_own, coef_sib = solve_pair(own(0), sib(0), proj_own, proj_sib, work_ref)
    put_wide(coef_ref, 0, coef_own)
    left = jnp.concatenate([proj_own + coef_sib, proj_sib + coef_own], 0)
    right = jnp.concatenate([coef_own, coef_sib], 0)
    at = 0
    for row_no in reversed(range(level_no)):
        order = [row_no] + list(range(row_no)) + [level_no]
        picked = [right[:, m_no * K : (m_no + 1) * K] for m_no in order]
        row = mtm(left[:, row_no * K : (row_no + 1) * K], jnp.concatenate(picked, 1))
        for m_no, field in enumerate(row_order(row_no)):
            next_ref[at] = both(row_no, field) - row[:, m_no * K : (m_no + 1) * K]
            at += 1
    if send_ref is not None:
        below = level_no - 1
        first = pl.multiple_of(core_no * HALF, HALF)
        row_no, column_no = grid_of(HALF, first)
        extra = jnp.zeros((8, K), jnp.float32)
        extra_row, _ = grid_of(8)
        extras = 0

        def some(row, m_no):
            return next_ref[full_index(below, row, m_no), pl.ds(first, HALF)]

        entries = packed_order(below)
        for at, entry in enumerate(entries):
            if entry[0] == "one":
                value = some(entry[1], entry[1])
            elif entry[0] == "pair":
                value = jnp.where(
                    column_no <= row_no,
                    some(entry[1], entry[1]),
                    some(entry[2], entry[2]),
                )
                lost = next_ref[full_index(below, entry[2], entry[2])]
                extra = jnp.where(extra_row == extras, diagonal_of(lost), extra)
                extras += 1
            else:
                value = some(*entry)
            send_ref[at * HALF : (at + 1) * HALF] = value
        send_ref[len(entries) * HALF :] = extra


def unpack(level_no, order, packed_ref, base, diagonals):
    found = {}
    pairs = 0
    for at, entry in enumerate(order):
        value = packed_ref[base + at]
        if entry[0] == "one":
            found[entry[1], entry[1]] = value
        elif entry[0] == "pair":
            found[entry[1], entry[1]] = from_lower(value)
            found[entry[2], entry[2]] = from_upper(value, diagonals[pairs])
            pairs += 1
        else:
            found[entry] = value
    return found


def join_halves(core_no, count, half_ref, far_ref, packed_ref, half_of):
    own = pl.ds(pl.multiple_of(core_no * HALF, HALF), HALF)
    far = pl.ds(pl.multiple_of((1 - core_no) * HALF, HALF), HALF)
    for at in range(count):
        packed_ref[at, own] = half_of(half_ref, at)
        packed_ref[at, far] = half_of(far_ref, at)


def finest_body(
    core_ref, half_ref, far_ref, next_ref, send_ref, coef_ref, work_ref, packed_ref
):
    level_no = LEVELS - 1
    core_no = core_ref[0]
    count = level_no + 2
    join_halves(
        core_no,
        half_ref.shape[1],
        half_ref,
        far_ref,
        packed_ref,
        lambda ref, at: ref[:, at].reshape(HALF, K),
    )
    diagonals = found_diagonals(packed_ref[0] + packed_ref[count])
    order = packed_order(level_no)
    both = unpack(level_no, order[count:], packed_ref, 2 * count, diagonals)
    eliminate(
        level_no,
        core_no,
        lambda m_no: packed_ref[m_no] if m_no else from_lower(packed_ref[0]),
        lambda m_no: packed_ref[count + m_no] if m_no else from_lower(packed_ref[count]),
        lambda row_no, field: both[row_no, field],
        next_ref,
        send_ref,
        coef_ref,
        work_ref,
    )


def middle_body(level_no, core_ref, own_ref, half_ref, far_ref, next_ref, *refs):
    send_ref, coef_ref, work_ref, packed_ref = refs if len(refs) == 4 else (None,) + refs
    core_no = core_ref[0]
    order = packed_order(level_no)
    join_halves(
        core_no,
        len(order),
        half_ref,
        far_ref,
        packed_ref,
        lambda ref, at: ref[at * HALF : (at + 1) * HALF],
    )
    tail = half_ref[len(order) * HALF :]
    found = unpack(level_no, order, packed_ref, 0, (tail[0:1], tail[1:2]))
    fields = row_order(level_no)
    eliminate(
        level_no,
        core_no,
        lambda m_no: own_ref[m_no],
        lambda m_no: found[level_no, fields[m_no]],
        lambda row_no, field: own_ref[full_index(level_no, row_no, field)]
        + found[row_no, field],
        next_ref,
        send_ref,
        coef_ref,
        work_ref,
    )


def fold_body(level_no, core_ref, coef_ref, *refs):
    finer = LEVELS - 1 - level_no
    coef = wide_of(coef_ref, 0, level_no + 1)
    for at in range(finer):
        old_ref, new_ref = refs[at], refs[finer + at]
        kept = list(range(level_no)) + [level_no + 1]
        old = jnp.concatenate([old_ref[m_no] for m_no in kept], 1)
        put_wide(new_ref, 0, old - mm(old_ref[level_no], coef))


def tail_body(core_ref, coef_ref, bases_ref, targets_ref, *refs):
    olds, (base_ref, rest_ref) = refs[:-2], refs[-2:]
    coef = wide_of(coef_ref, 0, 2)
    mults = [coef]
    for old_ref in reversed(olds):
        old = jnp.concatenate([old_ref[0], old_ref[2]], 1)
        mults.append(old - mm(old_ref[1], coef))
    tall = two_parts(jnp.concatenate(mults, 0))
    rows = targets_ref.shape[0]
    block = 256
    for first in range(0, rows, block):
        some = pl.ds(first, block)
        wide = [bases_ref[level_no, some] for level_no in range(1, LEVELS)]
        wide = two_parts(jnp.concatenate(wide, 1))
        taken = dot_parts(wide, tall, ((1,), (0,)))
        base_ref[some] = bases_ref[0, some] - taken[:, :K]
        rest_ref[some] = targets_ref[some] - taken[:, K:]


def coarsest_body(core_ref, own_ref, sib_ref, base_ref, rest_ref, out_ref, work_ref):
    inverse = inverse_of_complement(mm(sib_ref[0], own_ref[0]), work_ref)
    coef = mm(inverse, sib_ref[1] - mm(sib_ref[0], own_ref[1]))
    taken = dot_parts(two_parts(base_ref[...]), two_parts(coef), ((1,), (0,)))
    out_ref[...] = rest_ref[...] - taken


def swap(value, axis, partner):
    pairs = [(source, partner(source)) for source in range(lax.axis_size(axis))]
    return lax.ppermute(value, axis, pairs)


def swap_cores(value):
    return swap(value, "c", lambda at: at ^ 1)


PARTNERS = {
    4: ("x", lambda at: at ^ 1),
    3: ("x", lambda at: 3 - at),
    2: ("z", lambda at: at ^ 1),
    1: ("z", lambda at: at ^ 2),
    0: ("z", lambda at: (6, 7, 4, 5, 2, 3, 0, 1)[at]),
}
WORK = (2, K, K)


def sent_shape(level_no):
    return (len(packed_order(level_no)) * HALF + 8, K)


def per_device(bases, targets):
    top = LEVELS - 1
    head = top + 2
    core = lax.axis_index("c").astype(jnp.int32).reshape(1)
    keep, send = local_grams(core, bases, targets)
    part = keep + swap_cores(send)
    part = lax.all_to_all(part, "y", 0, 0).sum(0)
    other = swap(part, *PARTNERS[top])
    piece = jnp.concatenate([part[:head], other[:head], part[head:] + other[head:]], 0)
    half = gather_chips(piece)
    far = swap_cores(half)
    below = rows_up_to(top - 1)
    own, send, coef = call(
        finest_body,
        [(below, K, K), sent_shape(top - 1), (top + 1, K, K)],
        core,
        half,
        far,
        scratch=[WORK, (piece.shape[0], K, K)],
    )
    mults = [coef]
    folded = []
    for level_no in range(top - 1, 0, -1):
        half = swap(send, *PARTNERS[level_no])
        far = swap_cores(half)
        below = rows_up_to(level_no - 1)
        shapes = [(below, K, K), sent_shape(level_no - 1), (level_no + 1, K, K)]
        if level_no == 1:
            del shapes[1]
        outs = call(
            functools.partial(middle_body, level_no),
            shapes,
            core,
            own,
            half,
            far,
            scratch=[WORK, (len(packed_order(level_no)), K, K)],
            after=folded,
        )
        own, send, coef = outs[0], outs[-2], outs[-1]
        if level_no > 1:
            folded = call(
                functools.partial(fold_body, level_no),
                [(level_no + 1, K, K)] * len(mults),
                core,
                coef,
                *mults,
            )
            mults = folded + [coef]
    sib = swap(own, *PARTNERS[0])
    base, rest = call(
        tail_body, [targets.shape, targets.shape], core, coef, bases, targets, *mults
    )
    (solved,) = call(
        coarsest_body, [targets.shape], core, own, sib, base, rest, scratch=[WORK]
    )
    return solved


def gather_chips(piece):
    copies = jnp.broadcast_to(piece.reshape(1, -1, K), (CHIPS, piece.size // K, K))
    return lax.all_to_all(copies, "y", 0, 0).reshape((CHIPS,) + piece.shape)


def solution(mesh):
    split = Mesh(mesh.devices.reshape(SIZES), AXES)
    return jax.shard_map(
        per_device,
        mesh=split,
        in_specs=(P(None, AXES, None), P(AXES, None)),
        out_specs=P(AXES, None),
        check_vma=False,
    )
```

```python
import functools

import jax
import jax.numpy as jnp
from jax import lax
from jax.experimental import pallas as pl
from jax.experimental.pallas import tpu as pltpu
from jax.sharding import Mesh
from jax.sharding import PartitionSpec as P

LEVELS = 5
K = 128
HALF = K // 2
AXES = ("z", "x1", "x0", "y", "c")
SIZES = (8, 2, 2, 8, 2)
X_AXES = ("x1", "x0")
PAIR_AXES = ("x0", "y")
VMEM_SPEC = pl.BlockSpec(memory_space=pltpu.VMEM)
SMEM_SPEC = pl.BlockSpec(memory_space=pltpu.SMEM)

CHIPS = 8
TILE = HALF // CHIPS
TOTAL = 18


def rows_up_to(level_no):
    return sum(below + 2 for below in range(level_no + 1))


def row_order(level_no):
    return [level_no] + list(range(level_no)) + [LEVELS]


def packed_order(level_no):
    tops = [level_no] if level_no % 2 else [level_no - 1]
    pairs = [("pair", top, top - 1) for top in range(tops[0], 0, -2)]
    diagonals = pairs if level_no % 2 else [("one", level_no)] + pairs
    others = [
        [(row_no, m_no) for m_no in row_order(row_no)[1:]]
        for row_no in reversed(range(level_no + 1))
    ]
    return diagonals[:1] + others[0] + diagonals[1:] + sum(others[1:], [])


def full_index(level_no, row_no, m_no):
    above = sum(row + 2 for row in range(row_no + 1, level_no + 1))
    return above + row_order(row_no).index(m_no)


def grid_of(rows, first=0):
    row_no = lax.broadcasted_iota(jnp.int32, (rows, K), 0) + first
    return row_no, lax.broadcasted_iota(jnp.int32, (rows, K), 1)


def diagonal_of(matrix):
    row_no, column_no = grid_of(K)
    return jnp.sum(jnp.where(row_no == column_no, matrix, 0.0), 0, keepdims=True)


def from_lower(packed):
    row_no, column_no = grid_of(K)
    strict = jnp.where(column_no < row_no, packed, 0.0)
    return jnp.where(column_no <= row_no, packed, 0.0) + strict.T


def from_upper(packed, diagonal):
    row_no, column_no = grid_of(K)
    strict = jnp.where(column_no > row_no, packed, 0.0)
    return strict + strict.T + jnp.where(column_no == row_no, diagonal, 0.0)


def two_parts(value):
    high = value.astype(jnp.bfloat16)
    return high, (value - high.astype(jnp.float32)).astype(jnp.bfloat16)


def dot_parts(left, right, dims):
    dot = functools.partial(
        lax.dot_general, dimension_numbers=(dims, ((), ())), preferred_element_type=jnp.float32
    )
    return dot(left[0], right[0]) + (dot(left[0], right[1]) + dot(left[1], right[0]))


def mm(left, right):
    return dot_parts(two_parts(left), two_parts(right), ((1,), (0,)))


def mtm(left, right):
    return dot_parts(two_parts(left), two_parts(right), ((0,), (0,)))


GRANT = pltpu.CompilerParams(vmem_limit_bytes=16 * 2**20)


def call(body, out_shapes, core, *args, scratch=(), after=()):
    used = len(args) + 1

    def whole_body(*refs):
        body(*refs[:used], *refs[used + len(after) :])

    outs = pl.pallas_call(
        whole_body,
        out_shape=[jax.ShapeDtypeStruct(shape, jnp.float32) for shape in out_shapes],
        in_specs=[SMEM_SPEC]
        + [VMEM_SPEC] * len(args)
        + [pl.BlockSpec(memory_space=pl.ANY)] * len(after),
        out_specs=[VMEM_SPEC] * len(out_shapes),
        scratch_shapes=[pltpu.VMEM(shape, jnp.float32) for shape in scratch],
        compiler_params=GRANT,
    )(core, *args, *after)
    return list(outs)


GROUPS = (((4, 3), (4, 3, 2, 1, 0, 5)), ((2, 1), (2, 1, 0, 5)), ((0,), (0, 5)))


HEAD = LEVELS + 1


def owner_of(at):
    if at < HEAD:
        return at % 2, at // 2
    return (at - HEAD) % 2, HEAD // 2 + (at - HEAD) // 2


def hidden_diagonals(made):
    row_no, column_no = grid_of(K)
    out = jnp.zeros((K, K), jnp.float32)
    for pair_no, level_no in enumerate((2, 0)):
        diagonal = jnp.broadcast_to(diagonal_of(made[level_no, level_no]), (K, K))
        left = pltpu.roll(diagonal, HALF, 1)
        out = jnp.where(row_no == 2 * pair_no, left, out)
        out = jnp.where(row_no == 2 * pair_no + 1, diagonal, out)
    return jnp.where(column_no >= HALF, out, 0.0)


def found_diagonals(packed):
    _, column_no = grid_of(8)
    found = []
    for pair_no in range(2):
        left = jnp.broadcast_to(packed[2 * pair_no : 2 * pair_no + 1], (8, K))
        right = jnp.broadcast_to(packed[2 * pair_no + 1 : 2 * pair_no + 2], (8, K))
        both = jnp.where(column_no < HALF, pltpu.roll(left, HALF, 1), right)
        found.append(both[:1])
    return found


def gram_body(core_ref, bases_ref, targets_ref, keep_ref, send_ref):
    first = core_ref[0] == 0
    parts = [two_parts(bases_ref[level_no]) for level_no in range(LEVELS)]
    parts.append(two_parts(targets_ref[...]))

    def wide(fields):
        return [jnp.concatenate([parts[m_no][i] for m_no in fields], 1) for i in range(2)]

    made = {}
    for lefts, rights in GROUPS:
        block = dot_parts(wide(lefts), wide(rights), ((0,), (0,)))
        for top, level_no in enumerate(lefts):
            for field in row_order(level_no):
                to = rights.index(field)
                made[level_no, field] = block[top * K : (top + 1) * K, to * K : (to + 1) * K]
    row_no, column_no = grid_of(K)
    lower = column_no <= row_no
    for at, entry in enumerate(packed_order(LEVELS - 1)):
        if entry[0] == "one":
            value = jnp.where(lower, made[entry[1], entry[1]], hidden_diagonals(made))
        elif entry[0] == "pair":
            value = jnp.where(lower, made[entry[1], entry[1]], made[entry[2], entry[2]])
        else:
            value = made[entry]
        low = value[:HALF].reshape(CHIPS, TILE, K)
        high = value[HALF:].reshape(CHIPS, TILE, K)
        side, to = owner_of(at)
        keep_ref[side, :, to] = jnp.where(first, low, high)
        send_ref[side, :, to] = jnp.where(first, high, low)


def local_grams(core, bases, targets):
    shape = (2, CHIPS, TOTAL // 2, TILE, K)
    return call(gram_body, [shape, shape], core, bases, targets)


def inverse_of_complement(product, work_ref):
    row_no = lax.broadcasted_iota(jnp.int32, (K, K), 0)
    column_no = lax.broadcasted_iota(jnp.int32, (K, K), 1)
    eye = (row_no == column_no).astype(jnp.float32)

    def factor(power, inverse):
        power = mm(power, power)
        return power, inverse + mm(inverse, power)

    def size(value):
        return jnp.sum(value * value)

    power, inverse = product, eye + product
    for _ in range(3):
        power, inverse = factor(power, inverse)
    work_ref[0] = power
    work_ref[1] = inverse

    def more(carry):
        step, square = carry
        return (step < 64) & (square * square > 1e-20)

    def body(carry):
        power, inverse = factor(work_ref[0], work_ref[1])
        work_ref[0] = power
        work_ref[1] = inverse
        return carry[0] + 1, size(power)

    lax.while_loop(more, body, (jnp.int32(0), size(power)))
    return work_ref[1]


def solve_pair(gram_own, gram_sib, proj_own, proj_sib, work_ref):
    inverse = inverse_of_complement(mm(gram_sib, gram_own), work_ref)
    coef_own = mm(inverse, proj_sib - mm(gram_sib, proj_own))
    coef_sib = proj_own - mm(gram_own, coef_own)
    return coef_own, coef_sib


def wide_of(ref, first, count):
    return jnp.concatenate([ref[first + m_no] for m_no in range(count)], 1)


def put_wide(ref, first, value):
    for m_no in range(value.shape[1] // K):
        ref[first + m_no] = value[:, m_no * K : (m_no + 1) * K]


def eliminate(level_no, core_no, own, sib, both, next_ref, send_ref, coef_ref, work_ref):
    count = level_no + 1
    proj_own = jnp.concatenate([own(1 + m_no) for m_no in range(count)], 1)
    proj_sib = jnp.concatenate([sib(1 + m_no) for m_no in range(count)], 1)
    coef_own, coef_sib = solve_pair(own(0), sib(0), proj_own, proj_sib, work_ref)
    put_wide(coef_ref, 0, coef_own)
    left = jnp.concatenate([proj_own + coef_sib, proj_sib + coef_own], 0)
    right = jnp.concatenate([coef_own, coef_sib], 0)
    at = 0
    for row_no in reversed(range(level_no)):
        order = [row_no] + list(range(row_no)) + [level_no]
        picked = [right[:, m_no * K : (m_no + 1) * K] for m_no in order]
        row = mtm(left[:, row_no * K : (row_no + 1) * K], jnp.concatenate(picked, 1))
        for m_no, field in enumerate(row_order(row_no)):
            next_ref[at] = both(row_no, field) - row[:, m_no * K : (m_no + 1) * K]
            at += 1
    if send_ref is not None:
        below = level_no - 1
        first = pl.multiple_of(core_no * HALF, HALF)
        row_no, column_no = grid_of(HALF, first)
        extra = jnp.zeros((8, K), jnp.float32)
        extra_row, _ = grid_of(8)
        extras = 0

        def some(row, m_no):
            return next_ref[full_index(below, row, m_no), pl.ds(first, HALF)]

        entries = packed_order(below)
        for at, entry in enumerate(entries):
            if entry[0] == "one":
                value = some(entry[1], entry[1])
            elif entry[0] == "pair":
                value = jnp.where(
                    column_no <= row_no,
                    some(entry[1], entry[1]),
                    some(entry[2], entry[2]),
                )
                lost = next_ref[full_index(below, entry[2], entry[2])]
                extra = jnp.where(extra_row == extras, diagonal_of(lost), extra)
                extras += 1
            else:
                value = some(*entry)
            send_ref[at * HALF : (at + 1) * HALF] = value
        send_ref[len(entries) * HALF :] = extra


def unpack(level_no, order, packed_ref, base, diagonals):
    found = {}
    pairs = 0
    for at, entry in enumerate(order):
        value = packed_ref[base + at]
        if entry[0] == "one":
            found[entry[1], entry[1]] = value
        elif entry[0] == "pair":
            found[entry[1], entry[1]] = from_lower(value)
            found[entry[2], entry[2]] = from_upper(value, diagonals[pairs])
            pairs += 1
        else:
            found[entry] = value
    return found


def join_halves(core_no, count, half_ref, far_ref, packed_ref, half_of):
    own = pl.ds(pl.multiple_of(core_no * HALF, HALF), HALF)
    far = pl.ds(pl.multiple_of((1 - core_no) * HALF, HALF), HALF)
    for at in range(count):
        packed_ref[at, own] = half_of(half_ref, at)
        packed_ref[at, far] = half_of(far_ref, at)


def finest_body(
    place_ref, half_ref, far_ref, next_ref, send_ref, coef_ref, work_ref, packed_ref
):
    level_no = LEVELS - 1
    core_no = place_ref[0]
    count = level_no + 2
    own = pl.ds(pl.multiple_of(core_no * HALF, HALF), HALF)
    far = pl.ds(pl.multiple_of((1 - core_no) * HALF, HALF), HALF)
    for at in range(TOTAL):
        side, source = owner_of(at)
        if at < HEAD:
            mine = place_ref[1] * HEAD + at
            moves = ((source, mine), (HEAD // 2 + source, HEAD + 2 * at - mine))
        else:
            moves = ((HEAD // 2 + source, HEAD + at),)
        for source, to in moves:
            packed_ref[to, own] = half_ref[side, :, source].reshape(HALF, K)
            packed_ref[to, far] = far_ref[side, :, source].reshape(HALF, K)
    diagonals = found_diagonals(packed_ref[0] + packed_ref[count])
    order = packed_order(level_no)
    both = unpack(level_no, order[count:], packed_ref, 2 * count, diagonals)
    eliminate(
        level_no,
        core_no,
        lambda m_no: packed_ref[m_no] if m_no else from_lower(packed_ref[0]),
        lambda m_no: packed_ref[count + m_no] if m_no else from_lower(packed_ref[count]),
        lambda row_no, field: both[row_no, field],
        next_ref,
        send_ref,
        coef_ref,
        work_ref,
    )


def middle_body(level_no, core_ref, own_ref, half_ref, far_ref, next_ref, *refs):
    send_ref, coef_ref, work_ref, packed_ref = refs if len(refs) == 4 else (None,) + refs
    core_no = core_ref[0]
    order = packed_order(level_no)
    join_halves(
        core_no,
        len(order),
        half_ref,
        far_ref,
        packed_ref,
        lambda ref, at: ref[at * HALF : (at + 1) * HALF],
    )
    tail = half_ref[len(order) * HALF :]
    found = unpack(level_no, order, packed_ref, 0, (tail[0:1], tail[1:2]))
    fields = row_order(level_no)
    eliminate(
        level_no,
        core_no,
        lambda m_no: own_ref[m_no],
        lambda m_no: found[level_no, fields[m_no]],
        lambda row_no, field: own_ref[full_index(level_no, row_no, field)]
        + found[row_no, field],
        next_ref,
        send_ref,
        coef_ref,
        work_ref,
    )


def fold_body(level_no, core_ref, coef_ref, *refs):
    finer = LEVELS - 1 - level_no
    coef = wide_of(coef_ref, 0, level_no + 1)
    for at in range(finer):
        old_ref, new_ref = refs[at], refs[finer + at]
        kept = list(range(level_no)) + [level_no + 1]
        old = jnp.concatenate([old_ref[m_no] for m_no in kept], 1)
        put_wide(new_ref, 0, old - mm(old_ref[level_no], coef))


def tail_body(core_ref, coef_ref, bases_ref, targets_ref, *refs):
    olds, (base_ref, rest_ref) = refs[:-2], refs[-2:]
    coef = wide_of(coef_ref, 0, 2)
    mults = [coef]
    for old_ref in reversed(olds):
        old = jnp.concatenate([old_ref[0], old_ref[2]], 1)
        mults.append(old - mm(old_ref[1], coef))
    tall = two_parts(jnp.concatenate(mults, 0))
    rows = targets_ref.shape[0]
    block = 256
    for first in range(0, rows, block):
        some = pl.ds(first, block)
        wide = [bases_ref[level_no, some] for level_no in range(1, LEVELS)]
        wide = two_parts(jnp.concatenate(wide, 1))
        taken = dot_parts(wide, tall, ((1,), (0,)))
        base_ref[some] = bases_ref[0, some] - taken[:, :K]
        rest_ref[some] = targets_ref[some] - taken[:, K:]


def coarsest_body(core_ref, own_ref, sib_ref, base_ref, rest_ref, out_ref, work_ref):
    inverse = inverse_of_complement(mm(sib_ref[0], own_ref[0]), work_ref)
    coef = mm(inverse, sib_ref[1] - mm(sib_ref[0], own_ref[1]))
    taken = dot_parts(two_parts(base_ref[...]), two_parts(coef), ((1,), (0,)))
    out_ref[...] = rest_ref[...] - taken


def swap(value, axis, partner):
    pairs = [(source, partner(source)) for source in range(lax.axis_size(axis))]
    return lax.ppermute(value, axis, pairs)


def swap_cores(value):
    return swap(value, "c", lambda at: at ^ 1)


PARTNERS = {
    3: (X_AXES, lambda at: 3 - at),
    2: ("z", lambda at: at ^ 1),
    1: ("z", lambda at: at ^ 2),
    0: ("z", lambda at: (6, 7, 4, 5, 2, 3, 0, 1)[at]),
}
WORK = (2, K, K)


def sent_shape(level_no):
    return (len(packed_order(level_no)) * HALF + 8, K)


def per_device(bases, targets):
    top = LEVELS - 1
    head = top + 2
    place = [lax.axis_index(axis).astype(jnp.int32) for axis in ("c", "x0")]
    core = jnp.stack(place)
    keep, send = local_grams(core, bases, targets)
    part = keep + swap_cores(send)
    part = part.reshape(2 * CHIPS, TOTAL // 2 * TILE, K)
    part = lax.all_to_all(part, PAIR_AXES, 0, 0)
    sums = part.reshape(2, CHIPS, TOTAL // 2, TILE, K).sum(1)
    mine = head // 2
    piece = jnp.concatenate([sums[0, :mine], sums[1, :mine], sums[0, mine:] + sums[1, mine:]], 0)
    half = gather_chips(piece)
    far = swap_cores(half)
    below = rows_up_to(top - 1)
    own, send, coef = call(
        finest_body,
        [(below, K, K), sent_shape(top - 1), (top + 1, K, K)],
        core,
        half,
        far,
        scratch=[WORK, (2 * piece.shape[0], K, K)],
    )
    mults = [coef]
    folded = []
    for level_no in range(top - 1, 0, -1):
        half = swap(send, *PARTNERS[level_no])
        far = swap_cores(half)
        below = rows_up_to(level_no - 1)
        shapes = [(below, K, K), sent_shape(level_no - 1), (level_no + 1, K, K)]
        if level_no == 1:
            del shapes[1]
        outs = call(
            functools.partial(middle_body, level_no),
            shapes,
            core,
            own,
            half,
            far,
            scratch=[WORK, (len(packed_order(level_no)), K, K)],
            after=folded,
        )
        own, send, coef = outs[0], outs[-2], outs[-1]
        if level_no > 1:
            folded = call(
                functools.partial(fold_body, level_no),
                [(level_no + 1, K, K)] * len(mults),
                core,
                coef,
                *mults,
            )
            mults = folded + [coef]
    sib = swap(own, *PARTNERS[0])
    base, rest = call(
        tail_body, [targets.shape, targets.shape], core, coef, bases, targets, *mults
    )
    (solved,) = call(
        coarsest_body, [targets.shape], core, own, sib, base, rest, scratch=[WORK]
    )
    return solved


def gather_chips(piece):
    copies = jnp.broadcast_to(piece.reshape(1, -1, K), (2 * CHIPS, piece.size // K, K))
    gathered = lax.all_to_all(copies, PAIR_AXES, 0, 0)
    return gathered.reshape((2, CHIPS) + piece.shape)


def solution(mesh):
    split = Mesh(mesh.devices.reshape(SIZES), AXES)
    return jax.shard_map(
        per_device,
        mesh=split,
        in_specs=(P(None, AXES, None), P(AXES, None)),
        out_specs=P(AXES, None),
        check_vma=False,
    )
```
